32 devices in a mesh: group: 8 (over y, x, core), member: 4 (over z).
Axes of the slice: x: 2, y: 2, z: 4, core: 2. Of those that a mesh axis runs over, the one named last changes fastest.
Arguments:
- tokens: bfloat16 [4096, 2048], P(('group', 'member')), may hold values from -6 to 6
- grad_out: bfloat16 [4096, 2048], P(('group', 'member')), may hold values from -6 to 6
- expert_ids: int32 [4096, 8], P(('group', 'member')), may hold values from 0 to 31, as said below
- pair_slot: int32 [4096, 8], P(('group', 'member')), may hold values from 0 to 47, as said below
- gate_weights: bfloat16 [4096, 8], P(('group', 'member')), may hold values from 0.049804688 to 1
- weight_gate: bfloat16 [32, 2048, 768], P(('group', 'member')), may hold values from -0.125 to 0.125
- weight_up: bfloat16 [32, 2048, 768], P(('group', 'member')), may hold values from -0.125 to 0.125
- weight_down: bfloat16 [32, 768, 2048], P(('group', 'member')), may hold values from -0.21875 to 0.21875
- saved_gate: bfloat16 [32, 1536, 768], P(('group', 'member')), may hold values from -6 to 6
- saved_up: bfloat16 [32, 1536, 768], P(('group', 'member')), may hold values from -6 to 6
Outputs:
- grad_tokens: bfloat16 [4096, 2048], P(('group', 'member'))
- grad_gates: bfloat16 [4096, 8], P(('group', 'member'))
- grad_weight_gate: bfloat16 [32, 2048, 768], P(('group', 'member'))
- grad_weight_up: bfloat16 [32, 2048, 768], P(('group', 'member'))
- grad_weight_down: bfloat16 [32, 768, 2048], P(('group', 'member'))
The draws below stay inside these ranges and needn't reach their ends.
Inputs may be any that keep to these rules, and one draw needn't show every extreme that they name: `expert_ids`: each token names 8 distinct experts, two in each of exactly 4 groups, the group of expert e being e // 4. The tokens of one device send at most 96 tokens to one group, and in every draw some group gets exactly 96 from every device. `pair_slot`: among one device's assignments to one expert the slots are distinct and run from 0 to their count less one, in no fixed order of tokens. In every draw some expert gets exactly 48 assignments from every device.
All inputs are finite; a program needn't handle non-finite values.
Results may differ from the reference program's by a relative error of at most 0.012.
Values may be sent and summed in bfloat16 or wider, within the bound.
A program may use at most 192 MiB of HBM per device.

```python
import math
import jax
import jax.numpy as jnp
from jax import lax

D = 2048
FF = 768
TOP = 8
GROUP_VISITS = 4
TOK_DEV = 128
GROUPS = 8
MEMBERS = 4
EXPERTS = 32
TOKENS = 4096
PAIR = 48
CAP = 1536
GROUP_SLOTS = 96


def routing_tables(key):
    base_key = jax.random.fold_in(key, 11)
    key_pop, key_hot, key_member, key_devices = jax.random.split(base_key, 4)
    expert_preference = jax.random.randint(key_pop, (GROUPS,), 0, 2048, dtype=jnp.int32)
    favored_group = jax.random.randint(key_hot, (), 0, GROUPS, dtype=jnp.int32)
    hot_member = jax.random.randint(key_member, (), 0, MEMBERS, dtype=jnp.int32)
    group_indices = jnp.arange(GROUPS, dtype=jnp.int32)
    member_range = jnp.arange(MEMBERS, dtype=jnp.int32)
    group_extra_score = expert_preference + jnp.where(group_indices == favored_group, 1 << 20, 0)

    def token_step(carry, token_key):
        group_total, expert_count = carry
        key_groups, key_experts = jax.random.split(token_key)
        group_jitter = jax.random.randint(key_groups, (GROUPS,), 0, 1024, dtype=jnp.int32)
        expert_noise = jax.random.randint(key_experts, (EXPERTS,), 0, 1024, dtype=jnp.int32)
        group_affinity = jnp.where(group_total < GROUP_SLOTS, group_extra_score + group_jitter - group_total * 1024, -(1 << 23)) * 64 + group_indices
        chosen_groups = lax.top_k(group_affinity, GROUP_VISITS)[1]
        chosen_experts = []
        chosen_slots = []
        for visit_number in range(GROUP_VISITS):
            group_pick = chosen_groups[visit_number]
            first_expert = group_pick * MEMBERS
            counts = lax.dynamic_slice(expert_count, (first_expert,), (MEMBERS,))
            noise_here = lax.dynamic_slice(expert_noise, (first_expert,), (MEMBERS,))
            hot_boost = jnp.where((group_pick == favored_group) & (member_range == hot_member), 1 << 22, 0)
            expert_score = jnp.where(counts < PAIR, noise_here - counts * 2048 + hot_boost, -(1 << 24)) * 64 + member_range
            picked = lax.top_k(expert_score, 2)[1]
            chosen_experts.append(first_expert + picked)
            chosen_slots.append(counts[picked])
            expert_count = expert_count.at[first_expert + picked].add(1)
            group_total = group_total.at[group_pick].add(1)
        return ((group_total, expert_count), (jnp.concatenate(chosen_experts), jnp.concatenate(chosen_slots)))

    def one_device(device_key):
        key_tokens, key_order = jax.random.split(device_key)
        start_carry = (jnp.zeros((GROUPS,), jnp.int32), jnp.zeros((EXPERTS,), jnp.int32))
        tables = lax.scan(token_step, start_carry, jax.random.split(key_tokens, TOK_DEV))[1]
        order = jax.random.permutation(key_order, TOK_DEV)
        return (tables[0][order], tables[1][order])
    experts_all, slots_all = jax.vmap(one_device)(jax.random.split(key_devices, EXPERTS))
    return (experts_all.reshape(TOKENS, TOP).astype(jnp.int32), slots_all.reshape(TOKENS, TOP).astype(jnp.int32))


def draw_expert_ids(key, part):
    return routing_tables(key)[0]


def draw_pair_slot(key, part):
    return routing_tables(key)[1]


def level_of(stream_key, shape, shards, low, top_value):
    def one(position, parts):
        steps = jax.random.uniform(jax.random.fold_in(jax.random.fold_in(stream_key, 6), position), (parts,), jnp.float32, low / len(shards), top_value / len(shards))
        return jnp.repeat(jnp.exp(steps), shape[position] // parts).reshape((-1,) + (1,) * (len(shape) - position - 1))

    gain = one(*shards[0])
    for cut in shards[1:]:
        gain = gain * one(*cut)
    return gain


def gaussian(stream_key, shape, deviation, reach, cuts=(), held_as=jnp.bfloat16):
    factor_of = level_of(stream_key, shape, cuts, -0.22, 0.18) if cuts else 1.0
    entries = jax.random.normal(stream_key, shape, jnp.float32) * deviation * factor_of
    return jnp.minimum(jnp.maximum(entries, -reach), reach).astype(held_as)


def setup_inputs(seed: int = 0) -> dict:
    key_of = jax.random.split(jax.random.key(seed), 11)
    tokens = gaussian(key_of[0], (TOKENS, D), 1.0, 6.0, ((0, 32),))
    grad_out = gaussian(key_of[1], (TOKENS, D), 1.0, 6.0, ((0, 32),))
    expert_ids = draw_expert_ids(jax.random.fold_in(key_of[10], 71), 0)
    pair_slot = draw_pair_slot(jax.random.fold_in(key_of[10], 71), 0)
    gate_weights = jnp.clip(jnp.exp(math.log(1.0) - 2.9996462 * jax.random.uniform(key_of[4], (TOKENS, TOP), jnp.float32) ** level_of(key_of[4], (TOKENS, TOP), ((0, 32),), -0.2, 0.2)), 0.049804688, 1.0).astype(jnp.bfloat16)
    weight_gate = gaussian(key_of[5], (EXPERTS, D, FF), D ** -0.5, 0.125, ((0, 32),))
    weight_up = gaussian(key_of[6], (EXPERTS, D, FF), D ** -0.5, 0.125, ((0, 32),))
    weight_down = gaussian(key_of[7], (EXPERTS, FF, D), FF ** -0.5, 0.21875, ((0, 32),))
    saved_gate = gaussian(key_of[8], (EXPERTS, CAP, FF), 1.0, 6.0, ((0, 32),))
    saved_up = gaussian(key_of[9], (EXPERTS, CAP, FF), 1.0, 6.0, ((0, 32),))
    return dict(tokens=tokens, grad_out=grad_out, expert_ids=expert_ids, pair_slot=pair_slot, gate_weights=gate_weights, weight_gate=weight_gate, weight_up=weight_up, weight_down=weight_down, saved_gate=saved_gate, saved_up=saved_up)


def expert_block(token_rows, grad_rows, route_gate, saved_pregate, saved_preup, weight_gate, weight_up, weight_down):
    pre_gate = saved_pregate.astype(jnp.float32)
    pre_up = saved_preup.astype(jnp.float32)
    gate_sigmoid = jax.nn.sigmoid(pre_gate)
    gate_swish = pre_gate * gate_sigmoid
    hidden = gate_swish * pre_up
    hidden_low = hidden.astype(jnp.bfloat16)
    route_scale = route_gate.astype(jnp.float32)[:, None]
    scaled_grads = (route_scale * grad_rows.astype(jnp.float32)).astype(jnp.bfloat16)
    down_grad = jnp.dot(hidden_low.T, scaled_grads, preferred_element_type=jnp.float32)
    back_hidden = jnp.dot(grad_rows, weight_down.T, preferred_element_type=jnp.float32)
    slot_gate = jnp.sum(hidden * back_hidden, axis=1).astype(jnp.bfloat16)
    hidden_grad = route_scale * back_hidden
    pregate_grad = (hidden_grad * pre_up * gate_sigmoid * (1.0 + pre_gate * (1.0 - gate_sigmoid))).astype(jnp.bfloat16)
    preup_grad = (hidden_grad * gate_swish).astype(jnp.bfloat16)
    gate_grad = jnp.dot(token_rows.T, pregate_grad, preferred_element_type=jnp.float32)
    up_grad = jnp.dot(token_rows.T, preup_grad, preferred_element_type=jnp.float32)
    slot_grad = (jnp.dot(pregate_grad, weight_gate.T, preferred_element_type=jnp.float32)
                 + jnp.dot(preup_grad, weight_up.T, preferred_element_type=jnp.float32)).astype(jnp.bfloat16)
    return slot_grad, slot_gate, gate_grad, up_grad, down_grad


def reference(tokens, grad_out, expert_ids, pair_slot, gate_weights, weight_gate, weight_up, weight_down, saved_gate, saved_up):
    route_total = TOKENS * TOP
    route_index = jnp.arange(route_total, dtype=jnp.int32)
    source = (route_index // TOP) // TOK_DEV
    flat_slot = (expert_ids.reshape(-1) * CAP + source * PAIR + pair_slot.reshape(-1)).astype(jnp.int32)
    slot_route = jnp.full((EXPERTS * CAP,), route_total, jnp.int32).at[flat_slot].set(route_index)
    gates_flat = gate_weights.reshape(-1)

    def expert_step(carry, expert):
        token_acc, term_acc = carry
        routes_here = lax.dynamic_slice(slot_route, (expert * CAP,), (CAP,))
        token_here = (routes_here // TOP).astype(jnp.int32)
        rows_here = jnp.take(tokens, token_here, axis=0, mode="fill", fill_value=0)
        grads_here = jnp.take(grad_out, token_here, axis=0, mode="fill", fill_value=0)
        gates_here = jnp.take(gates_flat, routes_here, axis=0, mode="fill", fill_value=0)
        slot_grad, slot_gate, gate_grad, up_grad, down_grad = expert_block(
            rows_here, grads_here, gates_here, saved_gate[expert], saved_up[expert],
            weight_gate[expert], weight_up[expert], weight_down[expert])
        token_acc = token_acc.at[token_here].add(slot_grad.astype(jnp.float32), mode="drop")
        term_acc = term_acc.at[routes_here].set(slot_gate.astype(jnp.float32), mode="drop")
        return (token_acc, term_acc), (gate_grad.astype(jnp.bfloat16), up_grad.astype(jnp.bfloat16), down_grad.astype(jnp.bfloat16))

    start_carry = (jnp.zeros((TOKENS, D), jnp.float32), jnp.zeros((route_total,), jnp.float32))
    final_carry, weight_grads = lax.scan(expert_step, start_carry, jnp.arange(EXPERTS, dtype=jnp.int32))
    token_acc, term_acc = final_carry
    return (token_acc.astype(jnp.bfloat16), term_acc.reshape(TOKENS, TOP).astype(jnp.bfloat16),
            weight_grads[0], weight_grads[1], weight_grads[2])
```

```python
import jax
import jax.numpy as jnp
from jax import lax
from jax.sharding import PartitionSpec as P

AXES = ("group", "member")
OVER_ROWS = (((0,), (0,)), ((), ()))
OVER_FEATURES = (((1,), (1,)), ((), ()))


def expert_block(
    token_rows,
    grad_rows,
    route_gate,
    saved_pregate,
    saved_preup,
    weight_gate,
    weight_up,
    weight_down,
):
    pre_gate = saved_pregate.astype(jnp.float32)
    pre_up = saved_preup.astype(jnp.float32)
    gate_sigmoid = jax.nn.sigmoid(pre_gate)
    gate_swish = pre_gate * gate_sigmoid
    hidden = gate_swish * pre_up
    hidden_low = hidden.astype(jnp.bfloat16)
    route_scale = route_gate.astype(jnp.float32)[:, None]
    scaled_grads = (route_scale * grad_rows.astype(jnp.float32)).astype(jnp.bfloat16)
    over_rows = (((0,), (0,)), ((), ()))
    over_features = (((1,), (1,)), ((), ()))
    down_grad = lax.dot_general(
        hidden_low, scaled_grads, over_rows, preferred_element_type=jnp.float32
    )
    back_hidden = lax.dot_general(
        grad_rows, weight_down, over_features, preferred_element_type=jnp.float32
    )
    slot_gate = jnp.sum(hidden * back_hidden, axis=1).astype(jnp.bfloat16)
    hidden_grad = route_scale * back_hidden
    pregate_grad = (
        hidden_grad * pre_up * gate_sigmoid * (1.0 + pre_gate * (1.0 - gate_sigmoid))
    ).astype(jnp.bfloat16)
    preup_grad = (hidden_grad * gate_swish).astype(jnp.bfloat16)
    gate_grad = lax.dot_general(
        token_rows, pregate_grad, over_rows, preferred_element_type=jnp.float32
    )
    up_grad = lax.dot_general(token_rows, preup_grad, over_rows, preferred_element_type=jnp.float32)
    slot_grad = (
        lax.dot_general(
            pregate_grad, weight_gate, over_features, preferred_element_type=jnp.float32
        )
        + lax.dot_general(preup_grad, weight_up, over_features, preferred_element_type=jnp.float32)
    ).astype(jnp.bfloat16)
    return (slot_grad, slot_gate, gate_grad, up_grad, down_grad)


def pair_body(
    tokens,
    grad_out,
    expert_ids,
    pair_slot,
    gate_weights,
    weight_gate,
    weight_up,
    weight_down,
    saved_gate,
    saved_up,
):
    groups = lax.axis_size("group")
    members = lax.axis_size("member")
    experts = groups * members
    tok_rows, model_width = tokens.shape
    route_count = expert_ids.shape[1]
    capacity = saved_gate.shape[1]
    pair_rows = capacity // experts
    token_range = jnp.arange(tok_rows, dtype=jnp.int32)
    dest = (expert_ids * pair_rows + pair_slot).reshape(-1)
    slot_token = (
        jnp.full((experts * pair_rows,), tok_rows, jnp.int32)
        .at[dest]
        .set(jnp.repeat(token_range, route_count))
    )
    send_rows = jnp.take(tokens, slot_token, axis=0, mode="fill", fill_value=0)
    send_grads = jnp.take(grad_out, slot_token, axis=0, mode="fill", fill_value=0)
    send_gates = (
        jnp.zeros((experts * pair_rows,), jnp.bfloat16).at[dest].set(gate_weights.reshape(-1))
    )
    expert_rows, expert_grads, expert_gates = (
        lax.all_to_all(send_rows, ("group", "member"), split_axis=0, concat_axis=0, tiled=True),
        lax.all_to_all(send_grads, ("group", "member"), split_axis=0, concat_axis=0, tiled=True),
        lax.all_to_all(send_gates, ("group", "member"), split_axis=0, concat_axis=0, tiled=True),
    )
    slot_grad, slot_gate, gate_total, up_total, down_total = expert_block(
        expert_rows,
        expert_grads,
        expert_gates,
        saved_gate[0],
        saved_up[0],
        weight_gate[0],
        weight_up[0],
        weight_down[0],
    )
    back_rows, back_terms = (
        lax.all_to_all(slot_grad, ("group", "member"), split_axis=0, concat_axis=0, tiled=True),
        lax.all_to_all(slot_gate, ("group", "member"), split_axis=0, concat_axis=0, tiled=True),
    )
    per_route = jnp.take(back_rows, dest, axis=0).reshape(tok_rows, route_count, model_width)
    grad_tokens = jnp.sum(per_route.astype(jnp.float32), axis=1).astype(jnp.bfloat16)
    grad_gates = jnp.take(back_terms, dest, axis=0).reshape(tok_rows, route_count)
    return (
        grad_tokens,
        grad_gates,
        gate_total[None].astype(jnp.bfloat16),
        up_total[None].astype(jnp.bfloat16),
        down_total[None].astype(jnp.bfloat16),
    )


def dense_body(
    tokens,
    grad_out,
    expert_ids,
    pair_slot,
    gate_weights,
    weight_gate,
    weight_up,
    weight_down,
    saved_gate,
    saved_up,
):
    groups = lax.axis_size("group")
    members = lax.axis_size("member")
    experts = groups * members
    me = lax.axis_index("group") * members + lax.axis_index("member")
    tok_rows, width = tokens.shape
    capacity = saved_gate.shape[1]
    pair = capacity // experts
    f32, bf16 = jnp.float32, jnp.bfloat16

    all_grads = lax.all_gather(grad_out, AXES, axis=0, tiled=True)
    meta = jnp.concatenate(
        [expert_ids.astype(bf16), pair_slot.astype(bf16), gate_weights], axis=1
    )
    all_meta = lax.all_gather(meta, AXES, axis=0, tiled=True)
    route = expert_ids.shape[1]
    all_meta = all_meta.reshape(experts, tok_rows, 3, route).astype(f32)
    mine = all_meta[:, :, 0] == me.astype(f32)
    slot = jnp.sum(jnp.where(mine, all_meta[:, :, 1] + 1.0, 0.0), axis=2) - 1.0
    gate = jnp.sum(jnp.where(mine, all_meta[:, :, 2], 0.0), axis=2)
    pick = slot[:, None, :] == jnp.arange(pair, dtype=f32)[None, :, None]
    route_scale = jnp.sum(jnp.where(pick, gate[:, None, :], 0.0), axis=2).reshape(capacity, 1)
    pick = pick.astype(bf16)

    def rows_of(x):
        x = x.reshape(experts, tok_rows, width)
        got = lax.dot_general(pick, x, (((2,), (1,)), ((0,), (0,))), preferred_element_type=f32)
        return got.astype(bf16).reshape(capacity, width)

    grad_rows = rows_of(all_grads)
    all_tokens = lax.all_gather(tokens, AXES, axis=0, tiled=True)

    a = saved_gate[0].astype(f32)
    b = saved_up[0].astype(f32)
    sig = jax.nn.sigmoid(a)
    swish = a * sig
    hidden = swish * b
    back_hidden = lax.dot_general(
        grad_rows, weight_down[0], OVER_FEATURES, preferred_element_type=f32
    )
    slot_gate = jnp.sum(hidden * back_hidden, axis=1).astype(bf16)
    hidden_grad = route_scale * back_hidden
    pregate = (hidden_grad * b * sig * (1.0 + a * (1.0 - sig))).astype(bf16)
    preup = (hidden_grad * swish).astype(bf16)
    slot_grad = (
        lax.dot_general(pregate, weight_gate[0], OVER_FEATURES, preferred_element_type=f32)
        + lax.dot_general(preup, weight_up[0], OVER_FEATURES, preferred_element_type=f32)
    ).astype(bf16)
    lanes = 128
    lane = (jnp.arange(lanes) == me).astype(bf16)
    tail = slot_gate[:, None] * lane[None, :]
    send = jnp.concatenate([slot_grad, tail], axis=1).reshape(experts, pair, width + lanes)
    dense = lax.dot_general(pick, send, (((1,), (1,)), ((0,), (0,))), preferred_element_type=f32)
    dense = dense.astype(bf16).reshape(experts * tok_rows, width + lanes)
    back = lax.psum_scatter(dense, AXES, scatter_dimension=0, tiled=True)

    scaled = (route_scale * grad_rows.astype(f32)).astype(bf16)
    down_grad = lax.dot_general(
        hidden.astype(bf16), scaled, OVER_ROWS, preferred_element_type=f32
    )
    token_rows = rows_of(all_tokens)
    gate_grad = lax.dot_general(token_rows, pregate, OVER_ROWS, preferred_element_type=f32)
    up_grad = lax.dot_general(token_rows, preup, OVER_ROWS, preferred_element_type=f32)

    grad_tokens = back[:, :width]
    terms = back[:, width:].astype(f32)
    hit = expert_ids[:, :, None] == jnp.arange(lanes, dtype=jnp.int32)[None, None, :]
    grad_gates = jnp.sum(jnp.where(hit, terms[:, None, :], 0.0), axis=2).astype(bf16)
    return (
        grad_tokens,
        grad_gates,
        gate_grad.astype(bf16)[None],
        up_grad.astype(bf16)[None],
        down_grad.astype(bf16)[None],
    )


def body(*args):
    devices = lax.axis_size("group") * lax.axis_size("member")
    if devices * args[0].shape[0] <= 4 * args[8].shape[1]:
        return dense_body(*args)
    return pair_body(*args)


def solution(mesh):
    flat, deep = P(AXES, None), P(AXES, None, None)
    return jax.shard_map(
        body,
        mesh=mesh,
        in_specs=(flat,) * 5 + (deep,) * 5,
        out_specs=(flat, flat, deep, deep, deep),
        check_vma=False,
    )
```

```python
import jax
import jax.numpy as jnp
from jax import lax
from jax.sharding import PartitionSpec as P

AXES = ("group", "member")
OVER_ROWS = (((0,), (0,)), ((), ()))
OVER_FEATURES = (((1,), (1,)), ((), ()))


def expert_block(
    token_rows,
    grad_rows,
    route_gate,
    saved_pregate,
    saved_preup,
    weight_gate,
    weight_up,
    weight_down,
):
    pre_gate = saved_pregate.astype(jnp.float32)
    pre_up = saved_preup.astype(jnp.float32)
    gate_sigmoid = jax.nn.sigmoid(pre_gate)
    gate_swish = pre_gate * gate_sigmoid
    hidden = gate_swish * pre_up
    hidden_low = hidden.astype(jnp.bfloat16)
    route_scale = route_gate.astype(jnp.float32)[:, None]
    scaled_grads = (route_scale * grad_rows.astype(jnp.float32)).astype(jnp.bfloat16)
    over_rows = (((0,), (0,)), ((), ()))
    over_features = (((1,), (1,)), ((), ()))
    down_grad = lax.dot_general(
        hidden_low, scaled_grads, over_rows, preferred_element_type=jnp.float32
    )
    back_hidden = lax.dot_general(
        grad_rows, weight_down, over_features, preferred_element_type=jnp.float32
    )
    slot_gate = jnp.sum(hidden * back_hidden, axis=1).astype(jnp.bfloat16)
    hidden_grad = route_scale * back_hidden
    pregate_grad = (
        hidden_grad * pre_up * gate_sigmoid * (1.0 + pre_gate * (1.0 - gate_sigmoid))
    ).astype(jnp.bfloat16)
    preup_grad = (hidden_grad * gate_swish).astype(jnp.bfloat16)
    gate_grad = lax.dot_general(
        token_rows, pregate_grad, over_rows, preferred_element_type=jnp.float32
    )
    up_grad = lax.dot_general(token_rows, preup_grad, over_rows, preferred_element_type=jnp.float32)
    slot_grad = (
        lax.dot_general(
            pregate_grad, weight_gate, over_features, preferred_element_type=jnp.float32
        )
        + lax.dot_general(preup_grad, weight_up, over_features, preferred_element_type=jnp.float32)
    ).astype(jnp.bfloat16)
    return (slot_grad, slot_gate, gate_grad, up_grad, down_grad)


def pair_body(
    tokens,
    grad_out,
    expert_ids,
    pair_slot,
    gate_weights,
    weight_gate,
    weight_up,
    weight_down,
    saved_gate,
    saved_up,
):
    groups = lax.axis_size("group")
    members = lax.axis_size("member")
    experts = groups * members
    tok_rows, model_width = tokens.shape
    route_count = expert_ids.shape[1]
    capacity = saved_gate.shape[1]
    pair_rows = capacity // experts
    token_range = jnp.arange(tok_rows, dtype=jnp.int32)
    dest = (expert_ids * pair_rows + pair_slot).reshape(-1)
    slot_token = (
        jnp.full((experts * pair_rows,), tok_rows, jnp.int32)
        .at[dest]
        .set(jnp.repeat(token_range, route_count))
    )
    send_rows = jnp.take(tokens, slot_token, axis=0, mode="fill", fill_value=0)
    send_grads = jnp.take(grad_out, slot_token, axis=0, mode="fill", fill_value=0)
    send_gates = (
        jnp.zeros((experts * pair_rows,), jnp.bfloat16).at[dest].set(gate_weights.reshape(-1))
    )
    expert_rows, expert_grads, expert_gates = (
        lax.all_to_all(send_rows, ("group", "member"), split_axis=0, concat_axis=0, tiled=True),
        lax.all_to_all(send_grads, ("group", "member"), split_axis=0, concat_axis=0, tiled=True),
        lax.all_to_all(send_gates, ("group", "member"), split_axis=0, concat_axis=0, tiled=True),
    )
    slot_grad, slot_gate, gate_total, up_total, down_total = expert_block(
        expert_rows,
        expert_grads,
        expert_gates,
        saved_gate[0],
        saved_up[0],
        weight_gate[0],
        weight_up[0],
        weight_down[0],
    )
    back_rows, back_terms = (
        lax.all_to_all(slot_grad, ("group", "member"), split_axis=0, concat_axis=0, tiled=True),
        lax.all_to_all(slot_gate, ("group", "member"), split_axis=0, concat_axis=0, tiled=True),
    )
    per_route = jnp.take(back_rows, dest, axis=0).reshape(tok_rows, route_count, model_width)
    grad_tokens = jnp.sum(per_route.astype(jnp.float32), axis=1).astype(jnp.bfloat16)
    grad_gates = jnp.take(back_terms, dest, axis=0).reshape(tok_rows, route_count)
    return (
        grad_tokens,
        grad_gates,
        gate_total[None].astype(jnp.bfloat16),
        up_total[None].astype(jnp.bfloat16),
        down_total[None].astype(jnp.bfloat16),
    )


def dense_body(
    tokens,
    grad_out,
    expert_ids,
    pair_slot,
    gate_weights,
    weight_gate,
    weight_up,
    weight_down,
    saved_gate,
    saved_up,
):
    groups = lax.axis_size("group")
    members = lax.axis_size("member")
    experts = groups * members
    me = lax.axis_index("group") * members + lax.axis_index("member")
    tok_rows, width = tokens.shape
    capacity = saved_gate.shape[1]
    pair = capacity // experts
    f32, bf16 = jnp.float32, jnp.bfloat16

    all_grads = lax.all_gather(grad_out, AXES, axis=0, tiled=True)
    meta = jnp.concatenate(
        [expert_ids.astype(bf16), pair_slot.astype(bf16), gate_weights], axis=1
    )
    all_meta = lax.all_gather(meta, AXES, axis=0, tiled=True)
    route = expert_ids.shape[1]
    all_meta = all_meta.reshape(experts, tok_rows, 3, route).astype(f32)
    mine = all_meta[:, :, 0] == me.astype(f32)
    slot = jnp.sum(jnp.where(mine, all_meta[:, :, 1] + 1.0, 0.0), axis=2) - 1.0
    gate = jnp.sum(jnp.where(mine, all_meta[:, :, 2], 0.0), axis=2)
    pick = slot[:, None, :] == jnp.arange(pair, dtype=f32)[None, :, None]
    route_scale = jnp.sum(jnp.where(pick, gate[:, None, :], 0.0), axis=2).reshape(capacity, 1)
    pick = pick.astype(bf16)

    def rows_of(x):
        x = x.reshape(experts, tok_rows, width)
        got = lax.dot_general(pick, x, (((2,), (1,)), ((0,), (0,))), preferred_element_type=f32)
        return got.astype(bf16).reshape(capacity, width)

    grad_rows = rows_of(all_grads)
    all_tokens = lax.all_gather(tokens, AXES, axis=0, tiled=True)

    a = saved_gate[0].astype(f32)
    b = saved_up[0].astype(f32)
    sig = jax.nn.sigmoid(a)
    swish = a * sig
    hidden = swish * b
    back_hidden = lax.dot_general(
        grad_rows, weight_down[0], OVER_FEATURES, preferred_element_type=f32
    )
    slot_gate = jnp.sum(hidden * back_hidden, axis=1).astype(bf16)
    hidden_grad = route_scale * back_hidden
    pregate = (hidden_grad * b * sig * (1.0 + a * (1.0 - sig))).astype(bf16)
    preup = (hidden_grad * swish).astype(bf16)
    slot_grad = (
        lax.dot_general(pregate, weight_gate[0], OVER_FEATURES, preferred_element_type=f32)
        + lax.dot_general(preup, weight_up[0], OVER_FEATURES, preferred_element_type=f32)
    ).astype(bf16)
    back = lax.all_to_all(slot_grad, AXES, split_axis=0, concat_axis=0, tiled=True)
    terms = lax.all_to_all(slot_gate, AXES, split_axis=0, concat_axis=0, tiled=True)

    scaled = (route_scale * grad_rows.astype(f32)).astype(bf16)
    down_grad = lax.dot_general(
        hidden.astype(bf16), scaled, OVER_ROWS, preferred_element_type=f32
    )
    token_rows = rows_of(all_tokens)
    gate_grad = lax.dot_general(token_rows, pregate, OVER_ROWS, preferred_element_type=f32)
    up_grad = lax.dot_general(token_rows, preup, OVER_ROWS, preferred_element_type=f32)

    dest = expert_ids * pair + pair_slot
    hit = dest[:, :, None] == jnp.arange(capacity, dtype=jnp.int32)[None, None, :]
    grad_gates = jnp.sum(jnp.where(hit, terms.astype(f32), 0.0), axis=2).astype(bf16)
    grad_tokens = lax.dot_general(
        jnp.any(hit, axis=1).astype(bf16), back, (((1,), (0,)), ((), ())), preferred_element_type=f32
    ).astype(bf16)
    return (
        grad_tokens,
        grad_gates,
        gate_grad.astype(bf16)[None],
        up_grad.astype(bf16)[None],
        down_grad.astype(bf16)[None],
    )


def body(*args):
    devices = lax.axis_size("group") * lax.axis_size("member")
    if devices * args[0].shape[0] <= 4 * args[8].shape[1]:
        return dense_body(*args)
    return pair_body(*args)


def solution(mesh):
    flat, deep = P(AXES, None), P(AXES, None, None)
    return jax.shard_map(
        body,
        mesh=mesh,
        in_specs=(flat,) * 5 + (deep,) * 5,
        out_specs=(flat, flat, deep, deep, deep),
        check_vma=False,
    )
```
